32 devices in a mesh: seq: 2 (over x), ctx: 4 (over y, core), head: 4 (over z).
Axes of the slice: x: 2, y: 2, z: 4, core: 2. Of those that a mesh axis runs over, the one named last changes fastest.
Arguments:
- tokens: bfloat16 [2, 512, 2048], P('seq', 'ctx'), may hold values from -6 to 6
- query_matrix: bfloat16 [2048, 4096], P(('seq', 'ctx'), 'head'), may hold values from -0.125 to 0.125
- key_matrix: bfloat16 [2048, 512], P(('seq', 'ctx'), 'head'), may hold values from -0.125 to 0.125
- value_matrix: bfloat16 [2048, 512], P(('seq', 'ctx'), 'head'), may hold values from -0.125 to 0.125
- output_matrix: bfloat16 [2048, 4096], P(('seq', 'ctx'), 'head'), may hold values from -2 to 2
- prenorm: bfloat16 [2048], P(('seq', 'ctx')), may hold values from 0.5 to 1.5
- midnorm: bfloat16 [2048], P(('seq', 'ctx')), may hold values from 0.5 to 1.5
- querynorm: bfloat16 [128], P(('seq', 'ctx')), may hold values from 0.5 to 1.5
- keynorm: bfloat16 [128], P(('seq', 'ctx')), may hold values from 0.5 to 1.5
- router_weight: bfloat16 [2048, 16], P(('seq', 'ctx')), may hold values from -0.125 to 0.125
- gate_weight: bfloat16 [2048, 16, 768], P('ctx', ('seq', 'head')), may hold values from -0.125 to 0.125
- up_weight: bfloat16 [2048, 16, 768], P('ctx', ('seq', 'head')), may hold values from -0.125 to 0.125
- down_weight: bfloat16 [2048, 16, 768], P('ctx', ('seq', 'head')), may hold values from -0.21875 to 0.21875
- routes: int32 [2, 512, 8], P('seq', ('ctx', 'head')), may hold values from 0 to 15, all different within a row; in each aligned block of 32 rows (0 to 31, 32 to 63, ..., all dimensions but the last counted through in order) at most 24 rows name the same one
- cotangent: float32 [2, 512, 2048], P('seq', ('ctx', 'head')), may hold values from -6 to 6
Outputs:
- block_out: bfloat16 [2, 512, 2048], P('seq', ('ctx', 'head'))
- tokens_grad: float32 [2, 512, 2048], P('seq', ('ctx', 'head'))
- grad_query: float32 [2048, 4096], P(('seq', 'ctx'), 'head')
- grad_key: float32 [2048, 512], P(('seq', 'ctx'), 'head')
- grad_value: float32 [2048, 512], P(('seq', 'ctx'), 'head')
- grad_output: float32 [2048, 4096], P(('seq', 'ctx'), 'head')
- grad_prenorm: float32 [2048], P(('seq', 'ctx', 'head'))
- grad_midnorm: float32 [2048], P(('seq', 'ctx', 'head'))
- grad_querynorm: float32 [128], P(('seq', 'ctx', 'head'))
- grad_keynorm: float32 [128], P(('seq', 'ctx', 'head'))
- grad_router: float32 [2048, 16], P(('seq', 'ctx', 'head'))
- grad_gate: float32 [2048, 16, 768], P('ctx', ('seq', 'head'))
- grad_up: float32 [2048, 16, 768], P('ctx', ('seq', 'head'))
- grad_down: float32 [2048, 16, 768], P('ctx', ('seq', 'head'))
The draws below stay inside these ranges and needn't reach their ends.
Inputs may be any that keep to these rules, and one draw needn't show every extreme that they name: `routes`: each row names 8 different experts. In each aligned block of 32 rows (the rows of one device) no expert is named by more than 24 rows, a bound that some block reaches.
All inputs are finite; a program needn't handle non-finite values.
Results may differ from the reference program's by a relative error of at most 0.025.
Values may be sent and summed in bfloat16 or wider, within the bound.
No kernel may reach another device: no remote copies, remote signals or barrier semaphores. Data moves between devices by JAX's collectives and lax.ppermute only.
A program may use at most 192 MiB of HBM per device.

```python
import math
import jax
import jax.numpy as jnp
import numpy as np
from jax import lax

D = 2048
QUERY_HEADS = 32
KEY_VALUE_HEADS = 4
HEAD_SIZE = 128
FF = 768
TOP = 8
SEQUENCE_COUNT = 2
SEQUENCE_LENGTH = 512
EXPERTS = 16
MOE_ROWS = 32
CAP = 24


def level_of(stream_key, extent, shards, low, largest):
    def one(axis_at, shards_of):
        steps = jax.random.uniform(jax.random.fold_in(jax.random.fold_in(stream_key, 6), axis_at), (shards_of,), jnp.float32, low / len(shards), largest / len(shards))
        return jnp.repeat(jnp.exp(steps), extent[axis_at] // shards_of).reshape((-1,) + (1,) * (len(extent) - axis_at - 1))

    loudness = one(*shards[0])
    for cut in shards[1:]:
        loudness = loudness * one(*cut)
    return loudness


def deal_out(rng, own, number, rows, count, top, most, lean):
    order = jax.random.permutation(rng, count)
    packed, ordinary = load_shares(count, rows * top, most, lean, True), load_shares(count, rows * top, most, lean, False)
    places = jnp.arange(count)

    def named(tallies, rotation):
        used = int((tallies > 0).sum())
        fixed = max(1, used // 4)
        passed = fixed + (places - fixed + rotation * (used - fixed)) % max(1, count - fixed)
        return jnp.zeros((count,), jnp.int32).at[order[jnp.where(places < fixed, places, passed)]].set(jnp.asarray(tallies, jnp.int32))

    tallies = jnp.where(number % 4 == 0, named(packed, number // 4), named(ordinary, number - number // 4 - 1))
    mixed = jax.random.permutation(jax.random.fold_in(own, 3), count)
    giver, receiver = mixed[0:count // 2 * 2:2], mixed[1:count // 2 * 2:2]
    room = jnp.minimum(tallies[giver] - 1, most - tallies[receiver]) // 2
    room = jnp.where((giver == order[0]) | (receiver == order[0]) | (tallies[receiver] == 0), 0, jnp.maximum(room, 0))
    passed = jax.random.randint(jax.random.fold_in(own, 4), (count // 2,), 0, 1 << 20) % (room + 1)
    tallies = tallies.at[giver].add(-passed).at[receiver].add(passed)
    members = jnp.searchsorted(jnp.cumsum(tallies), jnp.arange(rows * top), side="right").astype(jnp.int32)
    grid = members.reshape(top, rows).T
    grid = grid[jax.random.permutation(jax.random.fold_in(own, 1), rows)]
    rotation = jax.random.randint(jax.random.fold_in(own, 2), (rows, 1), 0, top)
    return jnp.take_along_axis(grid, (jnp.arange(top)[None, :] + rotation) % top, axis=1)


def load_shares(number_of, total, reach, slope, full):
    portions = [(1 << 20) // math.isqrt(grade ** slope) + 1 for grade in range(1, number_of + 1)]
    largest = reach if full else min(reach, max(-(-total // number_of), total * portions[0] // sum(portions)))
    least = 1 if total - largest >= number_of - 1 else 0
    counts, rest = [largest] + [least] * (number_of - 1), total - largest - least * (number_of - 1)
    while rest > 0:
        candidates = [i for i in range(1, number_of) if counts[i] < largest] or [i for i in range(1, number_of) if counts[i] < reach]
        mass, budget = sum([portions[i] for i in candidates]), rest
        for i in candidates:
            addition = min(reach - counts[i], max(1, budget * portions[i] // mass), rest)
            counts[i] = counts[i] + addition
            rest = rest - addition
    return np.array(counts)


def scatter_about(key, shape, scale, reach, shards=(), kind=jnp.bfloat16):
    values = jax.random.normal(key, shape, jnp.float32) * scale
    if len(shards) > 0:
        values = level_of(key, shape, shards, -0.22, 0.18) * values
    return jnp.clip(values, min=-reach, max=reach).astype(kind)


def setup_inputs(seed: int = 0) -> dict:
    splits = jax.random.split(jax.random.key(seed), 16)
    tokens = scatter_about(splits[0], (SEQUENCE_COUNT, SEQUENCE_LENGTH, D), 1.0, 6.0, ((0, 2), (1, 4)))
    query_matrix = scatter_about(splits[1], (D, QUERY_HEADS * HEAD_SIZE), D ** -0.5, 0.125, ((0, 8), (1, 4)))
    key_matrix = scatter_about(splits[2], (D, KEY_VALUE_HEADS * HEAD_SIZE), D ** -0.5, 0.125, ((0, 8), (1, 4)))
    value_matrix = scatter_about(splits[3], (D, KEY_VALUE_HEADS * HEAD_SIZE), D ** -0.5, 0.125, ((0, 8), (1, 4)))
    output_matrix = scatter_about(splits[4], (D, QUERY_HEADS * HEAD_SIZE), (QUERY_HEADS * HEAD_SIZE // 512) ** -0.5, 2.0, ((0, 8), (1, 4)))
    prenorm = jnp.clip(1.0 + 0.1 * jax.random.normal(splits[5], (D,), jnp.float32), 0.5, 1.5).astype(jnp.bfloat16)
    midnorm = jnp.clip(1.0 + 0.1 * jax.random.normal(splits[6], (D,), jnp.float32), 0.5, 1.5).astype(jnp.bfloat16)
    querynorm = jnp.clip(1.0 + 0.1 * jax.random.normal(splits[7], (HEAD_SIZE,), jnp.float32), 0.5, 1.5).astype(jnp.bfloat16)
    keynorm = jnp.clip(1.0 + 0.1 * jax.random.normal(splits[8], (HEAD_SIZE,), jnp.float32), 0.5, 1.5).astype(jnp.bfloat16)
    router_weight = scatter_about(splits[9], (D, EXPERTS), D ** -0.5, 0.125, ((0, 8),))
    gate_weight = scatter_about(splits[10], (D, EXPERTS, FF), D ** -0.5, 0.125, ((0, 4), (1, 8)))
    up_weight = scatter_about(splits[11], (D, EXPERTS, FF), D ** -0.5, 0.125, ((0, 4), (1, 8)))
    down_weight = scatter_about(splits[12], (D, EXPERTS, FF), FF ** -0.5, 0.21875, ((0, 4), (1, 8)))
    routes_keys = jax.random.split(jax.random.fold_in(splits[13], 1), SEQUENCE_COUNT * SEQUENCE_LENGTH // MOE_ROWS)
    routes_turns = jax.random.permutation(jax.random.fold_in(splits[13], 3), SEQUENCE_COUNT * SEQUENCE_LENGTH // MOE_ROWS)
    routes = jax.vmap(lambda own, number: deal_out(jax.random.fold_in(splits[13], 2), own, number, MOE_ROWS, EXPERTS, TOP, CAP, 1))(routes_keys, routes_turns).reshape((SEQUENCE_COUNT, SEQUENCE_LENGTH, TOP))
    cotangent = scatter_about(splits[14], (SEQUENCE_COUNT, SEQUENCE_LENGTH, D), 1.0, 6.0, ((0, 2), (1, 16)), jnp.float32)
    return {"tokens": tokens, "query_matrix": query_matrix, "key_matrix": key_matrix, "value_matrix": value_matrix, "output_matrix": output_matrix, "prenorm": prenorm, "midnorm": midnorm, "querynorm": querynorm, "keynorm": keynorm, "router_weight": router_weight, "gate_weight": gate_weight, "up_weight": up_weight, "down_weight": down_weight, "routes": routes, "cotangent": cotangent}


EPSILON = 1e-06
THETA = 1000000.0
TOP_PRECISION = lax.Precision.HIGHEST

@jax.custom_vjp
def low(v):
    return lax.optimization_barrier(v.astype(jnp.bfloat16)).astype(jnp.float32)

@jax.custom_vjp
def lower_backward(v):
    return v

def low_keep(v):
    return (low(v), None)

def low_pass(kept, grad):
    return (grad,)

def back_keep(v):
    return (v, None)

def back_low(kept, grad):
    return (low(grad),)
low.defvjp(low_keep, low_pass)
lower_backward.defvjp(back_keep, back_low)

def norm_rows(values, gain):
    inverse = lax.rsqrt(lax.optimization_barrier(jnp.mean(values * values, axis=-1, keepdims=True)) + EPSILON)
    return values * inverse * gain

def rotary(heads, positions):
    width = heads.shape[-1]
    half = width // 2
    freqs = THETA ** (-2.0 * jnp.arange(half, dtype=jnp.float32) / width)
    angles = positions.astype(jnp.float32)[:, None] * freqs[None, :]
    cosine = jnp.cos(angles)[:, None, :]
    sine = jnp.sin(angles)[:, None, :]
    first = heads[..., :half]
    second = heads[..., half:]
    return jnp.concatenate([first * cosine - second * sine, second * cosine + first * sine], axis=-1)

def attend(query, key, value):
    span = min(SEQUENCE_LENGTH, 1024)
    count = SEQUENCE_LENGTH // span
    scale = HEAD_SIZE ** (-0.5)
    key_place = jnp.arange(SEQUENCE_LENGTH, dtype=jnp.int32)

    def one_block(inputs):
        block, index = inputs
        scores = lower_backward(jnp.einsum('qrd,kd->rqk', block, key, precision=TOP_PRECISION) * scale)
        query_place = index * span + jnp.arange(span, dtype=jnp.int32)
        visible = key_place[None, :] <= query_place[:, None]
        expo = jnp.where(visible[None], jnp.exp(scores), 0.0)
        total = lax.optimization_barrier(jnp.sum(expo, axis=-1))
        numer = lower_backward(jnp.einsum('rqk,kd->rqd', low(expo), value, precision=TOP_PRECISION))
        return numer / total[..., None]
    blocks = query.reshape(count, span, query.shape[1], HEAD_SIZE)
    result = lax.map(jax.checkpoint(one_block), (blocks, jnp.arange(count, dtype=jnp.int32)))
    return result.transpose(0, 2, 1, 3).reshape(SEQUENCE_LENGTH, query.shape[1], HEAD_SIZE)

def layer(tokens, query_matrix, key_matrix, value_matrix, output_matrix, prenorm, midnorm, querynorm, keynorm, router_weight, gate_weight, up_weight, down_weight, routes):
    positions = jnp.arange(SEQUENCE_LENGTH, dtype=jnp.int32)
    repeat = QUERY_HEADS // KEY_VALUE_HEADS
    normalized_input = low(norm_rows(tokens, prenorm))
    query_before_norm = lower_backward(jnp.einsum('pei,in->pen', normalized_input, query_matrix, precision=TOP_PRECISION)).reshape(SEQUENCE_COUNT, SEQUENCE_LENGTH, QUERY_HEADS, HEAD_SIZE)
    key_before_norm = lower_backward(jnp.einsum('pei,in->pen', normalized_input, key_matrix, precision=TOP_PRECISION)).reshape(SEQUENCE_COUNT, SEQUENCE_LENGTH, KEY_VALUE_HEADS, HEAD_SIZE)
    value_before_rotary = lower_backward(jnp.einsum('pei,in->pen', normalized_input, value_matrix, precision=TOP_PRECISION)).reshape(SEQUENCE_COUNT, SEQUENCE_LENGTH, KEY_VALUE_HEADS, HEAD_SIZE)
    queries = low(rotary(norm_rows(query_before_norm, querynorm), positions))
    keys = low(rotary(norm_rows(key_before_norm, keynorm), positions))
    values = low(value_before_rotary)
    grouped = queries.reshape(SEQUENCE_COUNT, SEQUENCE_LENGTH, KEY_VALUE_HEADS, repeat, HEAD_SIZE).transpose(0, 2, 1, 3, 4).reshape(SEQUENCE_COUNT * KEY_VALUE_HEADS, SEQUENCE_LENGTH, repeat, HEAD_SIZE)
    keys_flat = keys.transpose(0, 2, 1, 3).reshape(SEQUENCE_COUNT * KEY_VALUE_HEADS, SEQUENCE_LENGTH, HEAD_SIZE)
    values_flat = values.transpose(0, 2, 1, 3).reshape(SEQUENCE_COUNT * KEY_VALUE_HEADS, SEQUENCE_LENGTH, HEAD_SIZE)

    def per_group(inputs):
        return attend(inputs[0], inputs[1], inputs[2])
    attention_result = lax.map(per_group, (grouped, keys_flat, values_flat))
    attention_result = low(attention_result.reshape(SEQUENCE_COUNT, KEY_VALUE_HEADS, SEQUENCE_LENGTH, repeat, HEAD_SIZE).transpose(0, 2, 1, 3, 4).reshape(SEQUENCE_COUNT, SEQUENCE_LENGTH, QUERY_HEADS * HEAD_SIZE))
    expert_mixture = lower_backward(jnp.einsum('utw,bw->utb', attention_result, output_matrix, precision=TOP_PRECISION))
    resid = tokens + expert_mixture
    inner = low(norm_rows(resid, midnorm)).reshape(SEQUENCE_COUNT * SEQUENCE_LENGTH, D)
    logits = jnp.dot(inner, router_weight, precision=TOP_PRECISION)
    choose = routes.reshape(SEQUENCE_COUNT * SEQUENCE_LENGTH, TOP)
    chosen = jnp.take_along_axis(logits, choose, axis=1)
    lifted = jnp.exp(chosen)
    gates = lifted / lax.optimization_barrier(jnp.sum(lifted, axis=-1, keepdims=True))
    blocks = SEQUENCE_COUNT * SEQUENCE_LENGTH // MOE_ROWS
    flags = (choose.reshape(blocks, MOE_ROWS * TOP)[:, :, None] == jnp.arange(EXPERTS, dtype=jnp.int32)[None, None, :]).astype(jnp.int32)
    slots = lax.optimization_barrier(jnp.sum((jnp.cumsum(flags, axis=1) - flags) * flags, axis=-1)).reshape(-1)
    block_index = jnp.repeat(jnp.arange(blocks, dtype=jnp.int32), MOE_ROWS * TOP)
    places = block_index * CAP + slots
    expert_ids = choose.reshape(-1)
    token_ids = jnp.repeat(jnp.arange(SEQUENCE_COUNT * SEQUENCE_LENGTH, dtype=jnp.int32), TOP)
    table = jnp.zeros((EXPERTS, blocks * CAP), jnp.int32).at[expert_ids, places].set(token_ids)
    weighting = jnp.zeros((EXPERTS, blocks * CAP), jnp.float32).at[expert_ids, places].set(gates.reshape(-1))

    def one_expert(carry, inputs):
        rows_index, row_weight, gate_part, up_part, down_part = inputs
        entering = lower_backward(inner[rows_index])
        gate_pre = lower_backward(jnp.dot(entering, gate_part, precision=TOP_PRECISION))
        up_pre = lower_backward(jnp.dot(entering, up_part, precision=TOP_PRECISION))
        hidden = low(jax.nn.silu(gate_pre) * up_pre)
        leaving = low(lower_backward(jnp.dot(hidden, down_part.T, precision=TOP_PRECISION)))
        return (carry.at[rows_index].add(leaving * row_weight[:, None]), None)
    moe, unused = lax.scan(jax.checkpoint(one_expert), jnp.zeros((SEQUENCE_COUNT * SEQUENCE_LENGTH, D), jnp.float32), (table, weighting, jnp.moveaxis(gate_weight, 1, 0), jnp.moveaxis(up_weight, 1, 0), jnp.moveaxis(down_weight, 1, 0)))
    return resid + moe.reshape(SEQUENCE_COUNT, SEQUENCE_LENGTH, D)

def reference(tokens, query_matrix, key_matrix, value_matrix, output_matrix, prenorm, midnorm, querynorm, keynorm, router_weight, gate_weight, up_weight, down_weight, routes, cotangent):
    floats = tuple((value.astype(jnp.float32) for value in (tokens, query_matrix, key_matrix, value_matrix, output_matrix, prenorm, midnorm, querynorm, keynorm, router_weight, gate_weight, up_weight, down_weight)))

    def forward(*params):
        return layer(*params, routes)
    output, pullback = jax.vjp(forward, *floats)
    grads = pullback(cotangent.astype(jnp.float32))
    return (output.astype(jnp.bfloat16), grads[0], grads[1], grads[2], grads[3], grads[4], grads[5], grads[6], grads[7], grads[8], grads[9], grads[10], grads[11], grads[12])
```

```python
import jax
import jax.numpy as jnp
from jax import lax
from jax.sharding import PartitionSpec as P

HEAD_SIZE = 128
EPSILON = 1e-06
THETA = 1000000.0
EXACT = lax.Precision.HIGHEST
BF = jnp.bfloat16
F32 = jnp.float32


def swap(v, dim):
    axis, mask = dim
    return lax.ppermute(v, axis, [(i, i ^ mask) for i in range(lax.axis_size(axis))])


def gather_dims(v, dims):
    for dim in dims:
        v = jnp.concatenate([v, swap(v, dim)], axis=0)
    return v


def scatter_dims(v, dims):
    for dim in reversed(dims):
        half = v.shape[0] // 2
        v = v[:half].astype(F32) + swap(v[half:].astype(BF), dim).astype(F32)
    return v


def exchange_dims(v, dims):
    count = v.shape[0]
    for j, dim in enumerate(dims):
        w = v.reshape((count >> (j + 1), 2, 1 << j) + v.shape[1:])
        w = jnp.stack([w[:, 0], swap(w[:, 1], dim)], axis=1)
        v = w.reshape(v.shape)
    return v


def gather_line(v, axis):
    return jnp.concatenate([v] + [swap(v, (axis, m)) for m in range(1, lax.axis_size(axis))], axis=0)


def scatter_line(v, axis):
    size = lax.axis_size(axis)
    rows = v.shape[0] // size
    total = v[:rows].astype(F32)
    for m in range(1, size):
        total = total + swap(v[m * rows : (m + 1) * rows].astype(BF), (axis, m)).astype(F32)
    return total


def dot(a, b):
    return jnp.dot(a, b, preferred_element_type=F32)


def dot_nt(a, b):
    return lax.dot_general(a, b, (((1,), (1,)), ((), ())), preferred_element_type=F32)


def dot_tn(a, b):
    return lax.dot_general(a, b, (((0,), (0,)), ((), ())), preferred_element_type=F32)


def mask_of(index, bits):
    return sum(bit for j, bit in enumerate(bits) if index >> j & 1)


def blocks_at(v, starts, width, axis):
    return jnp.concatenate([lax.dynamic_slice_in_dim(v, s, width, axis) for s in starts], axis=axis)


def pair(v):
    high = v.astype(BF)
    return jnp.concatenate([high, (v - high.astype(F32)).astype(BF)], axis=-1)


def body(
    tokens,
    query_matrix,
    key_matrix,
    value_matrix,
    output_matrix,
    prenorm,
    midnorm,
    querynorm,
    keynorm,
    router_weight,
    gate_weight,
    up_weight,
    down_weight,
    routes,
    cotangent,
):
    seq_n, ctx_n, head_n = lax.axis_size("seq"), lax.axis_size("ctx"), lax.axis_size("head")
    seq_i, ctx_i, head_i = lax.axis_index("seq"), lax.axis_index("ctx"), lax.axis_index("head")
    core = [("ctx", 1)]
    ydims = [("ctx", 1 << j) for j in range(1, ctx_n.bit_length() - 1)]
    xdims = [("seq", 1 << j) for j in range(seq_n.bit_length() - 1)]
    plane = seq_n * ctx_n
    place = seq_i * ctx_n + ctx_i

    def bits_of(dims):
        return [mask * (1 if axis == "ctx" else ctx_n) for axis, mask in dims]

    order_a = xdims + ydims + core
    order_b = ydims + xdims + core
    order_c = core + ydims + xdims

    length, width = tokens.shape[1:]
    quarter = length // head_n
    rows_per = query_matrix.shape[0]
    half = rows_per // 2
    experts = router_weight.shape[1]

    masks_a = [mask_of(i, bits_of(order_a)) for i in range(plane)]
    masks_b = [mask_of(i, bits_of(order_b)) for i in range(plane)]

    def to_near(v):
        starts = [(place ^ m) * rows_per for m in masks_a] + [(place ^ m) * rows_per + half for m in masks_b]
        return blocks_at(v, starts, half, 1)

    def index_in(value, bits):
        return sum(((value // bit) % 2) << j for j, bit in enumerate(bits))

    at_a, at_b = index_in(place, bits_of(order_a)), index_in(place, bits_of(order_b))

    def to_far(v):
        starts = []
        for block in range(plane):
            starts.append((index_in(block, bits_of(order_a)) ^ at_a) * half)
            starts.append((plane + (index_in(block, bits_of(order_b)) ^ at_b)) * half)
        return blocks_at(v, starts, half, 1)

    small = jnp.concatenate(
        [prenorm, midnorm, router_weight.reshape(-1), querynorm, keynorm], axis=0
    )
    small_all = gather_dims(small[None], order_c)
    small_far = blocks_at(small_all, [index_in(j, bits_of(order_c)) ^ index_in(place, bits_of(order_c)) for j in range(plane)], 1, 0)
    cut = [0, rows_per, 2 * rows_per, 2 * rows_per + router_weight.size]
    cut += [cut[-1] + querynorm.size, cut[-1] + querynorm.size + keynorm.size]
    pre_far, mid_far, router_far, query_gain, key_gain = [
        small_far[:, a:b].astype(F32).reshape(-1) for a, b in zip(cut[:-1], cut[1:])
    ]
    router_far = router_far.reshape(width, experts)
    pre_near = to_near(pre_far[None])

    qkv_own = jnp.concatenate([query_matrix, key_matrix, value_matrix], axis=1)

    def gather_weight(w):
        return jnp.concatenate(
            [gather_dims(w[:half], order_a), gather_dims(w[half:], order_b)], axis=0
        )

    qkv_near = gather_weight(qkv_own)
    out_near = gather_weight(output_matrix)

    dims_a, dims_b = xdims + ydims, ydims + xdims

    def spread(v):
        line = gather_line(v, "head")
        cut_at = line.shape[0] // 2
        return jnp.concatenate(
            [gather_dims(line[:cut_at], dims_a), gather_dims(line[cut_at:], dims_b)], axis=0
        ), line

    def collect(v):
        cut_at = v.shape[0] // 2
        line = jnp.concatenate(
            [scatter_dims(v[:cut_at], dims_a), scatter_dims(v[cut_at:], dims_b)], axis=0
        )
        return scatter_line(line, "head")

    picked = routes[0][:, :, None] == jnp.arange(experts, dtype=jnp.int32)[None, None, :]
    chosen = jnp.any(picked, axis=1)
    upstream = cotangent[0]
    lanes = 128
    marks = jnp.pad(chosen.astype(BF), ((0, 0), (0, lanes - experts)))
    cot_spread, unused = spread(jnp.concatenate([upstream.astype(BF), marks], axis=1))
    cot_all, marks_all = cot_spread[:, :width], cot_spread[:, width : width + experts]

    parts = ctx_n // 2
    part = ctx_i // 2
    depth = gate_weight.shape[0]
    hidden_size = gate_weight.shape[2]
    columns = gate_weight.shape[1] * hidden_size // parts
    ybits = [mask // 2 for axis, mask in ydims]

    def columns_of(w, which):
        start = which * columns
        return lax.dynamic_slice(
            w, (0, start // hidden_size, start % hidden_size), (depth, 1, columns)
        )[:, 0]

    def fetch_expert(w):
        pieces = jnp.stack([columns_of(w, part ^ mask_of(m, ybits)) for m in range(parts)], axis=0)
        pieces = exchange_dims(pieces, ydims)
        return gather_dims(pieces, core).reshape(2 * parts * depth, columns)

    gate_full, up_full, down_full = (fetch_expert(w) for w in (gate_weight, up_weight, down_weight))
    ctx_masks = [mask_of(i, [2 * b for b in ybits] + [1]) for i in range(ctx_n)]
    ctx_bits = [2 * b for b in ybits] + [1]

    def to_ctx(v):
        return blocks_at(v, [(ctx_i ^ m) * depth for m in ctx_masks], depth, 1)

    def from_ctx(v):
        me = index_in(ctx_i, ctx_bits)
        return blocks_at(v, [(index_in(j, ctx_bits) ^ me) * depth for j in range(ctx_n)], depth, 1)

    scale = HEAD_SIZE ** (-0.5)
    row_starts = [(head_i ^ m) * quarter for m in range(head_n)]
    rows = to_near(blocks_at(tokens[0], row_starts, quarter, 0).astype(F32))
    own_tokens = lax.dynamic_slice_in_dim(tokens[0], head_i * quarter, quarter, 0).astype(F32)
    spots = jnp.concatenate([s + jnp.arange(quarter, dtype=jnp.int32) for s in row_starts])
    positions = ctx_i * length + spots
    inverse = lax.rsqrt(jnp.mean(rows * rows, axis=-1, keepdims=True) + EPSILON)
    normed = (rows * inverse * pre_near).astype(BF)
    qkv_pre = dot(normed, qkv_near)
    query_width = query_matrix.shape[1]
    query_heads = query_width // HEAD_SIZE
    query_pre = qkv_pre[:, :query_width].reshape(length, query_heads, HEAD_SIZE)
    key_pre = qkv_pre[:, query_width : query_width + HEAD_SIZE]
    value_pre = qkv_pre[:, query_width + HEAD_SIZE :]

    freqs = THETA ** (-2.0 * jnp.arange(HEAD_SIZE // 2, dtype=F32) / HEAD_SIZE)
    angles = positions.astype(F32)[:, None] * freqs[None, :]
    cosine, sine = jnp.cos(angles), jnp.sin(angles)

    def rotate(v, sign):
        cos, sin = cosine, sine * sign
        if v.ndim == 3:
            cos, sin = cos[:, None], sin[:, None]
        first, second = jnp.split(v, 2, axis=-1)
        return jnp.concatenate([first * cos - second * sin, second * cos + first * sin], axis=-1)

    def unit(v):
        return lax.rsqrt(jnp.mean(v * v, axis=-1, keepdims=True) + EPSILON)

    def norm_back(grad, values, inv, gain):
        scaled = values * inv
        lifted = grad * gain
        return inv * (lifted - scaled * jnp.mean(lifted * scaled, axis=-1, keepdims=True)), grad * scaled

    query_inv, key_inv = unit(query_pre), unit(key_pre)
    queries = rotate(query_pre * query_inv * query_gain, 1.0).astype(BF)
    keys = rotate(key_pre * key_inv * key_gain, 1.0).astype(BF)
    kv_dims = ydims + core
    kv_masks = [mask_of(i, bits_of(kv_dims)) for i in range(ctx_n)]
    kv_all = gather_dims(jnp.concatenate([keys, value_pre.astype(BF)], axis=1), kv_dims)
    key_all, value_all = kv_all[:, :HEAD_SIZE], kv_all[:, HEAD_SIZE:]
    key_places = jnp.concatenate([(ctx_i ^ m) * length + spots for m in kv_masks])
    query_group = queries.transpose(1, 0, 2).reshape(query_heads * length, HEAD_SIZE)
    query_places = jnp.tile(positions, query_heads)
    visible = key_places[None, :] <= query_places[:, None]
    expo = jnp.where(visible, jnp.exp(dot_nt(query_group, key_all) * scale), 0.0)
    expo_low = expo.astype(BF)
    total = jnp.sum(expo, axis=-1, keepdims=True)
    attended_f = dot(expo_low, value_all) / total
    attended = (
        attended_f.astype(BF)
        .reshape(query_heads, length, HEAD_SIZE)
        .transpose(1, 0, 2)
        .reshape(length, query_width)
    )
    mixed = to_far(scatter_line(dot_nt(attended, out_near), "head"))
    resid = own_tokens + mixed
    mid_inv = unit(resid)
    resid_unit = resid * mid_inv
    inner = (resid_unit * mid_far).astype(BF)

    inner_all, inner_line = spread(inner)

    def gates_of(rows_in, marked):
        logits = dot(rows_in, router_far.astype(BF))
        lifted = jnp.where(marked, jnp.exp(logits), 0.0)
        return lifted / jnp.sum(lifted, axis=-1, keepdims=True)

    gates = gates_of(inner, chosen)
    expert = (seq_i * head_n + head_i) * gate_weight.shape[1] + part * columns // hidden_size
    mine = (jnp.arange(experts, dtype=jnp.int32) == expert).astype(F32)
    weight = jnp.sum(gates_of(inner_all, marks_all > 0.5) * mine, axis=-1, keepdims=True)
    inner_ctx, cot_ctx = to_ctx(inner_all), to_ctx(cot_all)
    hidden_base = dot(cot_ctx, down_full)
    gate_pre = dot(inner_ctx, gate_full)
    up_pre = dot(inner_ctx, up_full)
    sigmoid = jax.nn.sigmoid(gate_pre)
    activated = gate_pre * sigmoid
    hidden = activated * up_pre
    gate_view = jnp.sum(hidden_base * hidden, axis=-1, keepdims=True) * mine
    hidden_grad = hidden_base * weight
    hidden_low = (hidden * weight).astype(BF)
    gate_pre_grad = (hidden_grad * up_pre * sigmoid * (1.0 + gate_pre * (1.0 - sigmoid))).astype(BF)
    up_pre_grad = (hidden_grad * activated).astype(BF)
    routed = from_ctx(dot_nt(gate_pre_grad, gate_full) + dot_nt(up_pre_grad, up_full))
    views = jnp.pad(pair(gate_view), ((0, 0), (0, lanes - 2 * experts)))
    back = collect(jnp.concatenate([routed.astype(BF), views], axis=1))
    moe = collect(from_ctx(dot_nt(hidden_low, down_full)).astype(BF))
    block_out = (resid + moe).astype(BF)[None]

    def give_expert(left, right):
        part_sum = dot_tn(left, right).reshape(ctx_n, depth, columns)
        part_sum = scatter_dims(part_sum, core).astype(BF)
        pieces = exchange_dims(part_sum, ydims)
        back_at = index_in(part, ybits)
        far = blocks_at(pieces, [index_in(j, ybits) ^ back_at for j in range(parts)], 1, 0).astype(F32)
        far = far.reshape(gate_weight.shape[1], hidden_size // columns, depth, columns)
        return far.transpose(2, 0, 1, 3).reshape(gate_weight.shape)

    gate_sum = give_expert(inner_ctx, gate_pre_grad)
    up_sum = give_expert(inner_ctx, up_pre_grad)
    down_sum = give_expert(cot_ctx, hidden_low)

    view_own = back[:, width : width + experts] + back[:, width + experts : width + 2 * experts]
    logit_grad = gates * (view_own - jnp.sum(gates * view_own, axis=-1, keepdims=True))
    inner_grad = back[:, :width] + lax.dot_general(
        logit_grad, router_far, (((1,), (1,)), ((), ())), precision=EXACT
    )
    resid_grad, midnorm_part = norm_back(inner_grad, resid, mid_inv, mid_far)
    resid_grad = resid_grad + upstream
    midnorm_part = to_near(jnp.sum(midnorm_part, axis=0, keepdims=True))
    mixed_grad = to_near(resid_grad.astype(BF))
    per_row = width // quarter
    extras = jnp.concatenate([pair(logit_grad), midnorm_part.reshape(quarter, per_row).astype(BF)], axis=1)
    extras = jnp.pad(extras, ((0, 0), (0, lanes - extras.shape[1])))
    mixed_line = gather_line(jnp.concatenate([mixed_grad, extras], axis=1), "head")
    mixed_grad = mixed_line[:, :width]
    logit_line = mixed_line[:, width : width + 2 * experts]
    mid_line = mixed_line[:, width + 2 * experts : width + 2 * experts + per_row].astype(F32)
    mid_near = jnp.sum(mid_line.reshape(head_n, quarter, per_row), axis=0).reshape(1, width)

    def near_pieces(v):
        found = []
        for i in range(plane):
            m = mask_of(i, bits_of(order_c))
            a, b = masks_a.index(m), masks_b.index(m)
            found.append(jnp.concatenate([v[:, a * half : (a + 1) * half], v[:, (plane + b) * half : (plane + b + 1) * half]], axis=1))
        return jnp.stack(found, axis=0)

    slice_rows = rows_per // head_n
    inner_slices = jnp.stack(
        [
            lax.dynamic_slice_in_dim(inner_line, (place ^ mask_of(i, bits_of(order_c))) * rows_per + head_i * slice_rows, slice_rows, 1)
            for i in range(plane)
        ],
        axis=0,
    )
    mid_columns = -(-rows_per // length)
    mid_pieces = near_pieces(mid_near)[:, 0].astype(BF)
    mid_pieces = jnp.pad(mid_pieces, ((0, 0), (0, mid_columns * length - rows_per)))
    mid_pieces = mid_pieces.reshape(plane, length, mid_columns)
    message = jnp.concatenate(
        [
            near_pieces(mixed_grad),
            inner_slices,
            jnp.broadcast_to(logit_line[None], (plane,) + logit_line.shape),
            mid_pieces,
        ],
        axis=2,
    )
    message = exchange_dims(message, order_c)
    a, b = rows_per, rows_per + slice_rows
    mixed_plane = message[:, :, :a].reshape(plane * length, rows_per)
    inner_plane = message[:, :, a:b].reshape(plane * length, slice_rows).astype(F32)
    logit_plane = message[:, :, b : b + 2 * experts].reshape(plane * length, 2 * experts).astype(F32)
    logit_plane = logit_plane[:, :experts] + logit_plane[:, experts:]
    mid_own = jnp.sum(message[:, :, b + 2 * experts :].astype(F32), axis=0).reshape(-1)
    midnorm_out = lax.dynamic_slice_in_dim(mid_own, head_i * slice_rows, slice_rows, 0)
    router_out = lax.dot_general(inner_plane, logit_plane, (((0,), (0,)), ((), ())), precision=EXACT)
    attended_plane = gather_dims(attended, order_c)
    output_sum = dot_tn(mixed_plane, attended_plane)

    attended_grad = dot(mixed_grad, out_near)
    grad_group = (
        attended_grad.reshape(length, query_heads, HEAD_SIZE)
        .transpose(1, 0, 2)
        .reshape(query_heads * length, HEAD_SIZE)
    )
    delta = jnp.sum(grad_group * attended_f, axis=-1, keepdims=True) / total
    numer_grad = (grad_group / total).astype(BF)
    score_grad = (expo * (dot_nt(numer_grad, value_all) - delta)).astype(BF)
    query_total = (dot(score_grad, key_all) * scale).reshape(query_heads, length, HEAD_SIZE).transpose(1, 0, 2)
    key_part = dot_tn(score_grad, query_group) * scale
    value_part = dot_tn(expo_low, numer_grad)
    kv_grad = scatter_dims(jnp.concatenate([key_part, value_part], axis=1), kv_dims)
    query_pre_grad, query_gain_part = norm_back(rotate(query_total, -1.0), query_pre, query_inv, query_gain)
    key_pre_grad, key_gain_part = norm_back(rotate(kv_grad[:, :HEAD_SIZE], -1.0), key_pre, key_inv, key_gain)
    pre_grad = jnp.concatenate(
        [query_pre_grad.reshape(length, query_width), key_pre_grad, kv_grad[:, HEAD_SIZE:]], axis=1
    ).astype(BF)
    gain_parts = jnp.stack([jnp.sum(query_gain_part, axis=(0, 1)), jnp.sum(key_gain_part, axis=0)], axis=1)
    gain_parts = jnp.pad(gain_parts.astype(BF), ((0, 0), (0, lanes - 2)))

    normed_plane = exchange_dims(near_pieces(normed), order_c).reshape(plane * length, rows_per)
    pre_plane = gather_dims(jnp.concatenate([pre_grad, gain_parts], axis=1), order_c)
    qkv_width = pre_grad.shape[1]
    qkv_sum = dot_tn(normed_plane, pre_plane[:, :qkv_width])
    prenorm_part = jnp.sum(qkv_sum * qkv_own.astype(F32), axis=1) / prenorm.astype(F32)
    gains = jnp.sum(
        pre_plane[:, qkv_width : qkv_width + 2].astype(F32).reshape(plane, length, 2), axis=0
    )
    last = jnp.concatenate([prenorm_part, gains[:, 0], gains[:, 1]])[None]
    last = jnp.sum(gather_line(last, "head"), axis=0)
    tiny = querynorm.size // head_n
    prenorm_out = lax.dynamic_slice_in_dim(last, head_i * slice_rows, slice_rows, 0)
    querynorm_out = lax.dynamic_slice_in_dim(last, rows_per + (place * head_n + head_i) * tiny, tiny, 0)
    keynorm_out = lax.dynamic_slice_in_dim(last, rows_per + HEAD_SIZE + (place * head_n + head_i) * tiny, tiny, 0)

    normed_grad = to_far(scatter_line(dot_nt(pre_grad, qkv_near), "head"))
    rows_grad, unused = norm_back(normed_grad, own_tokens, unit(own_tokens), pre_far)
    tokens_grad = (resid_grad + rows_grad)[None]
    return (
        block_out,
        tokens_grad,
        qkv_sum[:, :query_width],
        qkv_sum[:, query_width : query_width + HEAD_SIZE],
        qkv_sum[:, query_width + HEAD_SIZE :],
        output_sum,
        prenorm_out,
        midnorm_out,
        querynorm_out,
        keynorm_out,
        router_out,
        gate_sum,
        up_sum,
        down_sum,
    )


def solution(mesh):
    both = ("seq", "ctx")
    every = ("seq", "ctx", "head")
    expert = P("ctx", ("seq", "head"), None)
    token = P("seq", ("ctx", "head"), None)
    return jax.shard_map(
        body,
        mesh=mesh,
        in_specs=(P("seq", "ctx", None),)
        + (P(both, "head"),) * 4
        + (P(both),) * 4
        + (P(both, None),)
        + (expert,) * 3
        + (token,) * 2,
        out_specs=(token, token)
        + (P(both, "head"),) * 4
        + (P(every),) * 4
        + (P(every, None),)
        + (expert,) * 3,
        check_vma=False,
    )
```

```python
import functools

import jax
import jax.numpy as jnp
from jax import lax
from jax.experimental import pallas as pl
from jax.experimental.pallas import tpu as pltpu
from jax.sharding import PartitionSpec as P

HEAD_SIZE = 128
EPSILON = 1e-06
THETA = 1000000.0
EXACT = lax.Precision.HIGHEST
BF = jnp.bfloat16
F32 = jnp.float32
LANES = 128
PAD = 16
INTERPRET = False
BOTH = ("seq", "ctx")


def like(shape, dtype):
    return jax.ShapeDtypeStruct(shape, dtype)


def call(kernel, outs, args, scratch=(), grid=None, in_specs=None, out_specs=None, flops=0):
    whole = pl.BlockSpec(memory_space=pltpu.VMEM)
    moved = sum(v.size * v.dtype.itemsize for v in args) + sum(
        o.size * jnp.dtype(o.dtype).itemsize for o in outs
    )
    extra = {} if grid is None else {"grid": grid}
    return pl.pallas_call(
        kernel,
        out_shape=tuple(outs),
        in_specs=in_specs or [whole] * len(args),
        out_specs=tuple(out_specs or [whole] * len(outs)),
        scratch_shapes=list(scratch),
        compiler_params=pltpu.CompilerParams(vmem_limit_bytes=60 * 1024 * 1024),
        cost_estimate=pl.CostEstimate(flops=flops, bytes_accessed=moved, transcendentals=0),
        interpret=INTERPRET,
        **extra,
    )(*args)


def swap(v, axis, mask):
    return lax.ppermute(v, axis, [(i, i ^ mask) for i in range(lax.axis_size(axis))])


def dot(a, b):
    return jnp.dot(a, b, preferred_element_type=F32)


def dot_nt(a, b):
    return lax.dot_general(a, b, (((1,), (1,)), ((), ())), preferred_element_type=F32)


def dot_tn(a, b):
    return lax.dot_general(a, b, (((0,), (0,)), ((), ())), preferred_element_type=F32)


def inverse_root(v):
    return lax.rsqrt(jnp.mean(v * v, axis=-1, keepdims=True) + EPSILON)


def turn(v, cos, sin):
    return v * cos + pltpu.roll(v, HEAD_SIZE // 2, 1) * sin


def turn_back(v, cos, sin):
    return v * cos - pltpu.roll(v, HEAD_SIZE // 2, 1) * sin


def norm_back(grad, values, gain):
    inv = inverse_root(values)
    scaled = values * inv
    lifted = grad * gain
    lowered = inv * (lifted - scaled * jnp.mean(lifted * scaled, axis=-1, keepdims=True))
    return lowered, grad * scaled


def place_of():
    return lax.axis_index("seq") * lax.axis_size("ctx") + lax.axis_index("ctx")


def at(index, width):
    return pl.ds(pl.multiple_of(index * width, width), width)


def qkv_kernel(count, joined, r, heads, *refs):
    tokens, cos, sin = refs[:3]
    weights = refs[3 : 3 + count]
    extras = weights if joined else refs[3 + count : 3 + 2 * count]
    rest = refs[3 + count * (1 if joined else 2) :]
    query, pair, pre, even, odd, gains, head_gains, router, unit = rest
    top = r if joined else 0
    values = tokens[...].astype(F32)
    unit[...] = values * inverse_root(values)
    gains[...] = jnp.zeros_like(gains)
    query_gain = jnp.zeros((1, HEAD_SIZE), F32)
    key_gain = jnp.zeros((1, HEAD_SIZE), F32)
    for i in range(count):
        spot = at(place_of() ^ i, r) if joined else pl.ds(0, r)
        extra = extras[i]
        gain = extra[top : top + 1, 0:r].astype(F32)
        block = (unit[:, spot] * gain).astype(BF)
        if joined:
            (odd if i % 2 else even)[i // 2] = block
        else:
            even[0] = block
        part = dot(block, weights[i][0:r, :])
        pre[...] = part if i == 0 else pre[...] + part
        gains[0:1, spot] = gain
        gains[1:2, spot] = extra[top + 1 : top + 2, 0:r].astype(F32)
        router[:, spot] = extra[top : top + PAD, r : 2 * r]
        query_gain += extra[top : top + 1, 2 * r : 2 * r + HEAD_SIZE].astype(F32)
        key_gain += extra[top + 1 : top + 2, 2 * r : 2 * r + HEAD_SIZE].astype(F32)
    head_gains[...] = jnp.zeros_like(head_gains)
    head_gains[0:1, :] = query_gain
    head_gains[1:2, :] = key_gain
    for h in range(heads + 1):
        cut = slice(h * HEAD_SIZE, (h + 1) * HEAD_SIZE)
        value = pre[:, cut]
        gain = query_gain if h < heads else key_gain
        turned = turn(value * inverse_root(value) * gain, cos[...], sin[...]).astype(BF)
        if h < heads:
            query[:, cut] = turned
        else:
            pair[:, :HEAD_SIZE] = turned
    pair[:, HEAD_SIZE:] = pre[:, (heads + 1) * HEAD_SIZE :].astype(BF)


def load_pairs(pairs, keys, values):
    length = pairs[0].shape[0]
    for i, ref in enumerate(pairs):
        keys[i * length : (i + 1) * length, :] = ref[:, :HEAD_SIZE]
        values[i * length : (i + 1) * length, :] = ref[:, HEAD_SIZE:]


def seen(length, count):
    ctx = lax.axis_index("ctx")
    lane = lax.broadcasted_iota(jnp.int32, (length, count * length), 1)
    row = lax.broadcasted_iota(jnp.int32, (length, count * length), 0)
    return ((lane // length) ^ ctx) * length + lane % length <= ctx * length + row


def attend_kernel(count, plane, head_n, *refs):
    query, rest = refs[0], refs[1:]
    pairs, rest = rest[:count], rest[count:]
    outs, rest = rest[:plane], rest[plane:]
    attended, own = rest[:2]
    sends = rest[2 : 1 + head_n]
    keys, values, mixed = rest[1 + head_n :]
    load_pairs(pairs, keys, values)
    length, width = query.shape
    visible = seen(length, count)
    scale = HEAD_SIZE ** (-0.5)
    for h in range(width // HEAD_SIZE):
        cut = slice(h * HEAD_SIZE, (h + 1) * HEAD_SIZE)
        expo = jnp.where(visible, jnp.exp(dot_nt(query[:, cut], keys[...]) * scale), 0.0)
        total = jnp.sum(expo, axis=-1, keepdims=True)
        attended[:, cut] = (dot(expo.astype(BF), values[...]) / total).astype(BF)
    r = outs[0].shape[0]
    for i in range(plane):
        spot = at(place_of() ^ i, r) if plane > 1 else pl.ds(0, r)
        mixed[:, spot] = dot_nt(attended[...], outs[i][...])
    quarter = length // head_n
    head = lax.axis_index("head")
    own[...] = mixed[at(head, quarter), :]
    for m in range(1, head_n):
        sends[m - 1][...] = mixed[at(head ^ m, quarter), :].astype(BF)


def gates_of(inner, router, marks):
    experts = router.shape[0]
    lifted = jnp.where(marks[:, :experts] > 0.5, jnp.exp(dot_nt(inner, router)), 0.0)
    return lifted / jnp.sum(lifted, axis=-1, keepdims=True)


def middle_kernel(head_n, tokens, gains, router, marks, own, *rest):
    arrived, (resid, inner, gates) = rest[: head_n - 1], rest[head_n - 1 :]
    quarter = own.shape[0]
    mixed = own[...]
    for ref in arrived:
        mixed = mixed + ref[...].astype(F32)
    value = tokens[at(lax.axis_index("head"), quarter), :].astype(F32) + mixed
    resid[...] = value
    inner[...] = (value * inverse_root(value) * gains[1:2, :]).astype(BF)
    gates[...] = jnp.zeros_like(gates)
    gates[:, : router.shape[0]] = gates_of(inner[...], router[...], marks[...].astype(F32))


def base_kernel(arrays, blocks, ctx_n, *refs):
    cots, rest = refs[:arrays], refs[arrays:]
    weights, (base, cot, marks) = rest[:ctx_n], rest[ctx_n:]
    width = cot.shape[1]
    ctx = lax.axis_index("ctx")

    @pl.when(pl.program_id(0) == 0)
    def _():
        rows = cot.shape[0] // len(blocks)
        for i, (which, start) in enumerate(blocks):
            cot[i * rows : (i + 1) * rows, :] = cots[which][start : start + rows, :width]
            marks[i * rows : (i + 1) * rows, :] = cots[which][start : start + rows, width:]

    depth = weights[0].shape[1]
    total = None
    for m in range(ctx_n):
        part = dot(cot[:, at(ctx ^ m, depth)], weights[m][0])
        total = part if total is None else total + part
    base[...] = total


def expert_kernel(count, ctx_n, per_device, parts, *refs):
    pieces, rest = refs[:count], refs[count:]
    marks, router, base = rest[:3]
    weights, rest = rest[3 : 3 + ctx_n], rest[3 + ctx_n :]
    inner, gate_grad, up_grad, low = rest[:4]
    sends = rest[4 : 4 + count]
    total, weight, view = rest[4 + count :]
    step = pl.program_id(0)
    ctx = lax.axis_index("ctx")
    width = inner.shape[1]
    length = pieces[0].shape[0]
    index = lax.axis_index("seq") * lax.axis_size("head") + lax.axis_index("head")
    expert = index * per_device + (ctx // 2) * per_device // parts

    @pl.when(step == 0)
    def _():
        for i, ref in enumerate(pieces):
            inner[i * length : (i + 1) * length, :] = ref[...]
        gates = gates_of(inner[...], router[...], marks[...].astype(F32))
        lane = lax.broadcasted_iota(jnp.int32, gates.shape, 1)
        own = jnp.sum(jnp.where(lane == expert, gates, 0.0), axis=-1, keepdims=True)
        weight[...] = jnp.broadcast_to(own, weight.shape)
        view[...] = jnp.zeros_like(view)
        total[...] = jnp.zeros_like(total)

    depth = weights[0].shape[1]
    gate_pre = up_pre = None
    for m in range(ctx_n):
        block = inner[:, at(ctx ^ m, depth)]
        gate_part, up_part = dot(block, weights[m][0]), dot(block, weights[m][1])
        gate_pre = gate_part if gate_pre is None else gate_pre + gate_part
        up_pre = up_part if up_pre is None else up_pre + up_part
    own = weight[:, 0:1]
    sigmoid = 1.0 / (1.0 + jnp.exp(-gate_pre))
    activated = gate_pre * sigmoid
    hidden = activated * up_pre
    view[...] += jnp.broadcast_to(jnp.sum(base[...] * hidden, axis=-1, keepdims=True), view.shape)
    hidden_grad = base[...] * own
    low[...] = (hidden * own).astype(BF)
    gate_grad[...] = (hidden_grad * up_pre * sigmoid * (1.0 + gate_pre * (1.0 - sigmoid))).astype(BF)
    up_grad[...] = (hidden_grad * activated).astype(BF)
    for m in range(ctx_n):
        total[:, at(ctx ^ m, depth)] += dot_nt(gate_grad[...], weights[m][0]) + dot_nt(
            up_grad[...], weights[m][1]
        )

    @pl.when(step == pl.num_programs(0) - 1)
    def _():
        experts = router.shape[0]
        lane = lax.broadcasted_iota(jnp.int32, view.shape, 1)
        high = view[...].astype(BF).astype(F32)
        tail = jnp.where(lane == expert, high, 0.0)
        tail = jnp.where(lane == experts + expert, view[...] - high, tail).astype(BF)
        for i, ref in enumerate(sends):
            cut = slice(i * length, (i + 1) * length)
            ref[:, :width] = total[cut, :].astype(BF)
            ref[:, width:] = tail[cut, :]


def weight_kernel(blocks, arrays, ctx_n, *refs):
    gate_grad, up_grad, low, inner, cot = refs[:5]
    weights, rest = refs[5 : 5 + ctx_n], refs[5 + ctx_n :]
    even, odd = rest[:2]
    sends = rest[2 : 2 + arrays]
    inner_t, cot_t, total = rest[2 + arrays :]
    step = pl.program_id(0)
    ctx = lax.axis_index("ctx")
    depth = weights[0].shape[1]

    @pl.when(step == 0)
    def _():
        inner_t[...] = inner[...].T
        cot_t[...] = cot[...].T
        total[...] = jnp.zeros_like(total)

    for m in range(ctx_n):
        out = odd if m % 2 else even
        rows = at(ctx ^ m, depth)
        total[:, at(ctx ^ m, depth)] += dot_nt(low[...], weights[m][0])
        out[m // 2, 0] = dot(inner_t[rows, :], gate_grad[...]).astype(out.dtype)
        out[m // 2, 1] = dot(inner_t[rows, :], up_grad[...]).astype(out.dtype)
        out[m // 2, 2] = dot(cot_t[rows, :], low[...]).astype(out.dtype)

    @pl.when(step == pl.num_programs(0) - 1)
    def _():
        rows = total.shape[0] // len(blocks)
        for i, (which, start) in enumerate(blocks):
            sends[which][start : start + rows, :] = total[i * rows : (i + 1) * rows, :].astype(BF)


def reduce_kernel(count, blocks, *refs):
    terms, own, sends = refs[:count], refs[count], refs[count + 1 :]
    rows = own.shape[0]
    for b in range(blocks):
        cut = slice(b * rows, (b + 1) * rows)
        total = terms[0][cut, :].astype(F32)
        for ref in terms[1:]:
            total = total + ref[cut, :].astype(F32)
        if b == 0:
            own[...] = total
        else:
            sends[b - 1][...] = total.astype(BF)


def reduce_blocks(terms, blocks):
    rows, width = terms[0].shape[0] // blocks, terms[0].shape[1]
    outs = [like((rows, width), F32)] + [like((rows, width), BF)] * (blocks - 1)
    found = call(functools.partial(reduce_kernel, len(terms), blocks), outs, terms)
    return found[0], found[1:]


def resid_kernel(head_n, experts, upstream, resid, gates, gains, router, own, *rest):
    arrived, (resid_grad, message, mid) = rest[: head_n - 1], rest[head_n - 1 :]
    total = own[...]
    for ref in arrived:
        total = total + ref[...].astype(F32)
    width = resid.shape[1]
    view = total[:, width:]
    view = view + pltpu.roll(view, LANES - experts, 1)
    gate = gates[...]
    logit_grad = gate * (view - jnp.sum(gate * view, axis=-1, keepdims=True))
    high = logit_grad.astype(BF)
    rest_low = (logit_grad - high.astype(F32)).astype(BF)
    back = dot(high[:, :experts], router[...]) + dot(rest_low[:, :experts], router[...])
    inner_grad = total[:, :width] + back
    lowered, scaled = norm_back(inner_grad, resid[...], gains[1:2, :])
    lowered = lowered + upstream[...]
    resid_grad[...] = lowered
    mid[...] = jnp.broadcast_to(jnp.sum(scaled, axis=0, keepdims=True), mid.shape)
    message[:, :width] = lowered.astype(BF)
    lane = lax.broadcasted_iota(jnp.int32, high.shape, 1)
    tail = jnp.where(lane < experts, logit_grad, 0.0)
    low_part = pltpu.roll(rest_low.astype(F32), experts, 1)
    tail = jnp.where((lane >= experts) & (lane < 2 * experts), low_part, high.astype(F32) * (tail != 0.0))
    message[:, width:] = tail.astype(BF)


def rows_in_order(pieces, target, width):
    head = lax.axis_index("head")
    quarter = pieces[0].shape[0]
    for m, ref in enumerate(pieces):
        target[at(head ^ m, quarter), :] = ref[:, :width]


def back_kernel(count, plane, head_n, *refs):
    pieces, rest = refs[:head_n], refs[head_n:]
    outs, rest = rest[:plane], rest[plane:]
    query, rest = rest[0], rest[1:]
    pairs, rest = rest[:count], rest[count:]
    pre, head_gains, cos, sin = rest[:4]
    query_grad, even, odd, gain_part = rest[4:8]
    keys, values, mixed, grads, key_sum, value_sum = rest[8:]
    load_pairs(pairs, keys, values)
    rows_in_order(pieces, mixed, mixed.shape[1])
    r = outs[0].shape[0]
    for i in range(plane):
        spot = at(place_of() ^ i, r) if plane > 1 else pl.ds(0, r)
        part = dot(mixed[:, spot], outs[i][...])
        grads[...] = part if i == 0 else grads[...] + part
    length, width = query.shape
    visible = seen(length, count)
    scale = HEAD_SIZE ** (-0.5)
    gain = head_gains[0:1, :]
    gain_sum = jnp.zeros((1, HEAD_SIZE), F32)
    for h in range(width // HEAD_SIZE):
        cut = slice(h * HEAD_SIZE, (h + 1) * HEAD_SIZE)
        head_query = query[:, cut]
        expo = jnp.where(visible, jnp.exp(dot_nt(head_query, keys[...]) * scale), 0.0)
        total = jnp.sum(expo, axis=-1, keepdims=True)
        numer_grad = (grads[:, cut] / total).astype(BF)
        expo_low = expo.astype(BF)
        prob_grad = dot_nt(numer_grad, values[...])
        delta = jnp.sum(expo_low.astype(F32) * prob_grad, axis=-1, keepdims=True) / total
        score_grad = (expo * (prob_grad - delta)).astype(BF)
        key_part, value_part = dot_tn(score_grad, head_query), dot_tn(expo_low, numer_grad)
        key_sum[...] = key_part if h == 0 else key_sum[...] + key_part
        value_sum[...] = value_part if h == 0 else value_sum[...] + value_part
        turned = turn_back(dot(score_grad, keys[...]) * scale, cos[...], sin[...])
        lowered, scaled = norm_back(turned, pre[:, cut], gain)
        query_grad[:, cut] = lowered.astype(BF)
        gain_sum += jnp.sum(scaled, axis=0, keepdims=True)
    gain_part[...] = jnp.broadcast_to(gain_sum, gain_part.shape)
    for m in range(count):
        cut = slice(m * length, (m + 1) * length)
        out = odd if m % 2 else even
        out[m // 2, :, :HEAD_SIZE] = (key_sum[cut, :] * scale).astype(BF)
        out[m // 2, :, HEAD_SIZE:] = value_sum[cut, :].astype(BF)


def join_kernel(arrived, *refs):
    query_grad, pre, head_gains, cos, sin, gain_part, mid, own = refs[:8]
    terms, (joined,) = refs[8 : 8 + arrived], refs[8 + arrived :]
    pair = own[...].astype(F32)
    for ref in terms:
        pair = pair + ref[...].astype(F32)
    width = query_grad.shape[1]
    turned = turn_back(pair[:, :HEAD_SIZE], cos[...], sin[...])
    lowered, scaled = norm_back(turned, pre[:, width : width + HEAD_SIZE], head_gains[1:2, :])
    joined[:, :width] = query_grad[...]
    joined[:, width : width + HEAD_SIZE] = lowered.astype(BF)
    joined[:, width + HEAD_SIZE : width + 2 * HEAD_SIZE] = pair[:, HEAD_SIZE:].astype(BF)
    tail = slice(width + 2 * HEAD_SIZE, width + 3 * HEAD_SIZE)
    joined[:, tail] = jnp.zeros((joined.shape[0], HEAD_SIZE), BF)
    key_part = jnp.sum(scaled, axis=0, keepdims=True)
    head_part = jnp.concatenate([gain_part[0:1, :], key_part, jnp.zeros((14, HEAD_SIZE), F32)], axis=0)
    joined[0:16, tail] = head_part.astype(BF)
    joined[16 : 16 + mid.shape[0], tail] = mid[...].astype(BF)


def normed_kernel(plane, joined_rows, head_n, *refs):
    grads, rest = refs[0], refs[1:]
    weights, rest = rest[:plane], rest[plane:]
    own, sends, normed = rest[0], rest[1:head_n], rest[head_n]
    r = joined_rows
    width = weights[0].shape[1]
    for i in range(plane):
        spot = at(place_of() ^ i, r) if plane > 1 else pl.ds(0, r)
        normed[:, spot] = dot_nt(grads[:, :width], weights[i][0:r, :])
    head = lax.axis_index("head")
    quarter = own.shape[0]
    own[...] = normed[at(head, quarter), :]
    for m in range(1, head_n):
        sends[m - 1][...] = normed[at(head ^ m, quarter), :].astype(BF)


def qkv_grad_kernel(count, r, top, plane, *refs):
    even, recv = refs[:2]
    far, rest = refs[2 : 2 + count], refs[2 + count :]
    grads, rest = rest[:plane], rest[plane:]
    weight, prenorm = rest[:2]
    query_out, key_out, value_out, last = rest[2:6]
    total = rest[6]
    width = weight.shape[1]
    tail = None
    for i in range(plane):
        block = (recv if i % 2 else even)[0] if i < 2 else far[i // 2 - 1][i % 2]
        part = dot_tn(block, grads[i][:, :width])
        total[...] = part if i == 0 else total[...] + part
        extra = grads[i][0:32, width:].astype(F32)
        tail = extra if tail is None else tail + extra
    heads_width = query_out.shape[1]
    query_out[...] = total[:, :heads_width]
    key_out[...] = total[:, heads_width : heads_width + HEAD_SIZE]
    value_out[...] = total[:, heads_width + HEAD_SIZE :]
    product = total[...] * weight[0:r, :].astype(F32)
    ones = jnp.ones((8, width), F32)
    row = lax.dot_general(
        ones, product, (((1,), (1,)), ((), ())), precision=EXACT, preferred_element_type=F32
    )[0:1, :]
    row = row / prenorm[...].astype(F32)
    last[...] = jnp.zeros_like(last)
    last[0:32, :] = tail
    for j in range(-(-r // LANES)):
        wide = min(LANES, r - j * LANES)
        last[32 + j : 33 + j, :wide] = row[:, j * LANES : j * LANES + wide]


def split_kernel(plane, head_n, experts, slices, *refs):
    pieces, line = refs[:head_n], refs[head_n]
    even, odd, mixed, inner, tail = refs[head_n + 1 :]
    width = mixed.shape[1]
    head = lax.axis_index("head")
    quarter = pieces[0].shape[0]
    rows_in_order(pieces, mixed, width)
    for m, ref in enumerate(pieces):
        tail[at(head ^ m, quarter), :] = ref[:, width:].astype(F32)
        inner[at(head ^ m, quarter), :] = line[m * quarter : (m + 1) * quarter, :]
    r = even.shape[2] - LANES
    lane = lax.broadcasted_iota(jnp.int32, tail.shape, 1)
    side = pltpu.roll(tail[...], slices, 1)
    for i in range(plane):
        out = odd if i % 2 else even
        spot = at(place_of() ^ i, r)
        out[i // 2, :, :r] = mixed[:, spot]
        near = pltpu.roll(inner[:, spot].astype(F32), r - head * slices, 1)[:, :LANES]
        out[i // 2, :, r:] = jnp.where(lane < slices, near, side).astype(BF)


def output_grad_kernel(count, r, plane, *refs):
    even, recv = refs[:2]
    far, rest = refs[2 : 2 + count], refs[2 + count :]
    attended, (out, small) = rest[:plane], rest[plane:]
    for i in range(plane):
        block = (recv if i % 2 else even)[0] if i < 2 else far[i // 2 - 1][i % 2]
        part = dot_tn(block[:, :r], attended[i][...])
        tail = block[:, r:]
        side = dot_tn(tail, tail)
        out[...] = part if i == 0 else out[...] + part
        small[...] = side if i == 0 else small[...] + side


def final_kernel(head_n, tokens, gains, resid_grad, own, *rest):
    arrived, (out,) = rest[: head_n - 1], rest[head_n - 1 :]
    total = own[...]
    for ref in arrived:
        total = total + ref[...].astype(F32)
    value = tokens[at(lax.axis_index("head"), own.shape[0]), :].astype(F32)
    lowered, unused = norm_back(total, value, gains[0:1, :])
    out[...] = resid_grad[...] + lowered


def body(
    tokens,
    query_matrix,
    key_matrix,
    value_matrix,
    output_matrix,
    prenorm,
    midnorm,
    querynorm,
    keynorm,
    router_weight,
    gate_weight,
    up_weight,
    down_weight,
    routes,
    cotangent,
):
    seq_n, ctx_n, head_n = lax.axis_size("seq"), lax.axis_size("ctx"), lax.axis_size("head")
    ctx_i, head_i = lax.axis_index("ctx"), lax.axis_index("head")
    place = place_of()
    plane = seq_n * ctx_n
    chips = plane // 2
    length, width = tokens.shape[1:]
    quarter = length // head_n
    r = query_matrix.shape[0]
    heads_width = query_matrix.shape[1]
    heads = heads_width // HEAD_SIZE
    experts = router_weight.shape[1]
    wide = r % LANES == 0

    def by_mask(v):
        near = [v] + [swap(v, BOTH, 2 * c) for c in range(1, chips)]
        return [w for n in near for w in (n, swap(n, BOTH, 1))]

    def line_of(v):
        return [v] + [swap(v, "head", m) for m in range(1, head_n)]

    def cross(even, odd):
        recv = swap(odd, BOTH, 1)
        far = [swap(jnp.stack([even[c], recv[c]]), BOTH, 2 * c) for c in range(1, chips)]
        return [even, recv] + far

    def in_order(pieces, axis):
        stacked = jnp.stack(pieces)
        return jnp.concatenate(
            [lax.dynamic_index_in_dim(stacked, place ^ j, 0, keepdims=False) for j in range(plane)], axis=axis
        )

    def placed(v):
        row = jnp.zeros((HEAD_SIZE,), v.dtype)
        return lax.dynamic_update_slice(row, v, (place * v.shape[0],))

    blank = jnp.zeros((PAD - 2, r), BF)
    extra = jnp.concatenate(
        [
            jnp.concatenate([prenorm[None], midnorm[None], blank], axis=0),
            jnp.pad(router_weight.T, ((0, PAD - experts), (0, 0))),
            jnp.concatenate([placed(querynorm)[None], placed(keynorm)[None], jnp.zeros((PAD - 2, HEAD_SIZE), BF)], axis=0),
        ],
        axis=1,
    )
    extra = jnp.pad(extra, ((0, 0), (0, heads_width + 2 * HEAD_SIZE - extra.shape[1])))
    qkv_own = jnp.concatenate(
        [jnp.concatenate([query_matrix, key_matrix, value_matrix], axis=1), extra], axis=0
    )
    qkv_pieces = by_mask(qkv_own)

    positions = ctx_i * length + jnp.arange(length, dtype=jnp.int32)
    freqs = THETA ** (-2.0 * jnp.arange(HEAD_SIZE // 2, dtype=F32) / HEAD_SIZE)
    angles = positions.astype(F32)[:, None] * freqs[None, :]
    cos = jnp.concatenate([jnp.cos(angles)] * 2, axis=1)
    sin = jnp.concatenate([-jnp.sin(angles), jnp.sin(angles)], axis=1)

    picked = routes[0][:, :, None] == jnp.arange(LANES, dtype=jnp.int32)[None, None, :]
    marks = jnp.any(picked, axis=1).astype(BF)
    upstream = cotangent[0]
    cot = jnp.concatenate([upstream.astype(BF), marks], axis=1)
    sides = ctx_n // 2
    cot = jnp.concatenate([cot] + [swap(cot, "ctx", 2 * y) for y in range(1, sides)], axis=0)
    cot = jnp.concatenate(line_of(cot), axis=0)
    cots = [cot] + [swap(cot, "seq", x) for x in range(1, seq_n)]

    parts, part = ctx_n // 2, ctx_i // 2
    depth, per_device, hidden_size = gate_weight.shape
    columns = per_device * hidden_size // parts
    split = hidden_size // columns
    stacked = jnp.stack([jnp.moveaxis(w, 1, 0) for w in (gate_weight, up_weight, down_weight)], axis=1)

    def columns_of(which):
        start = which * columns
        return lax.dynamic_slice(
            stacked, (start // hidden_size, 0, 0, start % hidden_size), (1, 3, depth, columns)
        )[0]

    expert_near = [columns_of(part)] + [swap(columns_of(part ^ y), "ctx", 2 * y) for y in range(1, parts)]
    expert_pieces = [w for n in expert_near for w in (n, swap(n, "ctx", 1))]
    out_pieces = by_mask(output_matrix)

    if wide:
        qkv_args, qkv_rows = qkv_pieces, r
        outs_args = out_pieces
        blocks_n = plane
    else:
        mains = in_order([p[:r] for p in qkv_pieces], 0)
        tails = [p[r:] for p in qkv_pieces]
        extra_all = jnp.concatenate(
            [
                in_order([t[:, :r] for t in tails], 1),
                in_order([t[:, r : 2 * r] for t in tails], 1),
                sum(t[:, 2 * r : 2 * r + HEAD_SIZE] for t in tails),
            ],
            axis=1,
        )
        qkv_args, qkv_rows = [mains, extra_all], width
        outs_args = [in_order(out_pieces, 0)]
        blocks_n = 1
    qkv_width = heads_width + 2 * HEAD_SIZE
    small_shape = like((max(chips, 1), length, r), BF) if wide else like((1, length, width), BF)
    query, pair, pre, even, odd, gains, head_gains, router = call(
        functools.partial(qkv_kernel, blocks_n, wide, qkv_rows, heads),
        [
            like((length, heads_width), BF),
            like((length, 2 * HEAD_SIZE), BF),
            like((length, qkv_width), F32),
            small_shape,
            small_shape,
            like((8, width), F32),
            like((8, HEAD_SIZE), F32),
            like((PAD, width), BF),
        ],
        [tokens[0], cos, sin] + qkv_args,
        scratch=[pltpu.VMEM((length, width), F32)],
    )
    router = router[:experts]
    if not wide:
        blocks = [lax.dynamic_slice_in_dim(even[0], (place ^ i) * r, r, 1) for i in range(plane)]
        even, odd = jnp.stack(blocks[0::2]), jnp.stack(blocks[1::2])
    pairs = [pair] + [swap(pair, "ctx", m) for m in range(1, ctx_n)]
    sends = [like((quarter, width), BF)] * (head_n - 1)
    kv_scratch = [pltpu.VMEM((ctx_n * length, HEAD_SIZE), BF)] * 2
    attended, mixed, *mixed_sends = call(
        functools.partial(attend_kernel, ctx_n, blocks_n, head_n),
        [like((length, heads_width), BF), like((quarter, width), F32)] + sends,
        [query] + pairs + outs_args,
        scratch=kv_scratch + [pltpu.VMEM((length, width), F32)],
    )
    arrived = [swap(v, "head", m + 1) for m, v in enumerate(mixed_sends)]
    resid, inner, gates = call(
        functools.partial(middle_kernel, head_n),
        [like((quarter, width), F32), like((quarter, width), BF), like((quarter, LANES), F32)],
        [tokens[0], gains, router, marks, mixed] + arrived,
    )

    inner_line = jnp.concatenate(line_of(inner), axis=0)
    inner_pieces = [inner_line] + [swap(inner_line, BOTH, 2 * c) for c in range(1, chips)]
    chunk = 256 if columns % 256 == 0 else columns
    steps = columns // chunk
    group = min(chips, 4)
    groups = chips // group
    rows_n = group * length
    whole = pl.BlockSpec(memory_space=pltpu.VMEM)

    def fixed(shape):
        return pl.BlockSpec(shape, lambda j: (0,) * len(shape))

    def by_column(rows):
        return pl.BlockSpec((rows, chunk), lambda j: (0, j))

    down_spec = pl.BlockSpec((1, depth, chunk), lambda j: (2, 0, j))
    both_spec = pl.BlockSpec((2, depth, chunk), lambda j: (0, 0, j))
    wide_row = width + LANES
    tokens_back, moe_back, weight_even, weight_odd = [], [], None, None
    for g in range(groups):
        own = range(g * group, (g + 1) * group)
        blocks = [
            (c // sides, (z * sides + c % sides) * quarter) for c in own for z in range(head_n)
        ]
        base, cot_all, marks_all = call(
            functools.partial(base_kernel, seq_n, blocks, ctx_n),
            [like((rows_n, columns), F32), like((rows_n, width), BF), like((rows_n, LANES), BF)],
            cots + expert_pieces,
            grid=(steps,),
            in_specs=[fixed(v.shape) for v in cots] + [down_spec] * ctx_n,
            out_specs=[by_column(rows_n), fixed((rows_n, width)), fixed((rows_n, LANES))],
        )
        found = call(
            functools.partial(expert_kernel, group, ctx_n, per_device, parts),
            [like((rows_n, width), BF)]
            + [like((rows_n, columns), BF)] * 3
            + [like((length, wide_row), BF)] * group,
            [inner_pieces[c] for c in own] + [marks_all, router, base] + expert_pieces,
            grid=(steps,),
            in_specs=[fixed((length, width))] * group
            + [fixed((rows_n, LANES)), fixed(router.shape), by_column(rows_n)]
            + [both_spec] * ctx_n,
            out_specs=[fixed((rows_n, width))]
            + [by_column(rows_n)] * 3
            + [fixed((length, wide_row))] * group,
            scratch=[
                pltpu.VMEM((rows_n, width), F32),
                pltpu.VMEM((rows_n, LANES), F32),
                pltpu.VMEM((rows_n, LANES), F32),
            ],
        )
        inner_all, gate_grad, up_grad, low = found[:4]
        tokens_back += found[4:]
        grad_type = BF if groups == 1 else F32
        local = [(0 if groups > 1 else which, start if groups == 1 else i * quarter) for i, (which, start) in enumerate(blocks)]
        back_n = seq_n if groups == 1 else 1
        grad_spec = pl.BlockSpec((ctx_n // 2, 3, depth, chunk), lambda j: (0, 0, 0, j))
        part_even, part_odd, *moe_sends = call(
            functools.partial(weight_kernel, local, back_n, ctx_n),
            [like((ctx_n // 2, 3, depth, columns), grad_type)] * 2
            + [like((rows_n // back_n, width), BF)] * back_n,
            [gate_grad, up_grad, low, inner_all, cot_all] + expert_pieces,
            grid=(steps,),
            in_specs=[by_column(rows_n)] * 3 + [fixed((rows_n, width))] * 2 + [down_spec] * ctx_n,
            out_specs=[grad_spec] * 2 + [fixed((rows_n // back_n, width))] * back_n,
            scratch=[
                pltpu.VMEM((width, rows_n), BF),
                pltpu.VMEM((width, rows_n), BF),
                pltpu.VMEM((rows_n, width), F32),
            ],
        )
        moe_back += moe_sends
        weight_even = part_even if weight_even is None else weight_even + part_even
        weight_odd = part_odd if weight_odd is None else weight_odd + part_odd
    if groups > 1:
        moe_all = jnp.concatenate(moe_back, axis=0).reshape(seq_n, sides, head_n, quarter, width)
        moe_all = moe_all.transpose(0, 2, 1, 3, 4).reshape(seq_n, -1, width)
        moe_back = [moe_all[x] for x in range(seq_n)]

    terms = [tokens_back[0]] + [swap(tokens_back[c], BOTH, 2 * c) for c in range(1, chips)]
    back, back_sends = reduce_blocks(terms, head_n)
    back_terms = [swap(v, "head", m + 1) for m, v in enumerate(back_sends)]

    resid_grad, message, mid = call(
        functools.partial(resid_kernel, head_n, experts),
        [like((quarter, width), F32), like((quarter, wide_row), BF), like((8, width), F32)],
        [upstream, resid, gates, gains, router, back] + back_terms,
    )
    mid = mid[0].reshape(width // LANES, LANES)
    pieces = line_of(message)

    pair_shape = like((ctx_n // 2, length, 2 * HEAD_SIZE), BF)
    query_grad, pair_even, pair_odd, gain_part = call(
        functools.partial(back_kernel, ctx_n, blocks_n, head_n),
        [like((length, heads_width), BF), pair_shape, pair_shape, like((8, HEAD_SIZE), F32)],
        pieces + outs_args + [query] + pairs + [pre, head_gains, cos, sin],
        scratch=kv_scratch
        + [
            pltpu.VMEM((length, width), BF),
            pltpu.VMEM((length, heads_width), F32),
            pltpu.VMEM((ctx_n * length, HEAD_SIZE), F32),
            pltpu.VMEM((ctx_n * length, HEAD_SIZE), F32),
        ],
    )
    pair_sum = pair_even.astype(F32) + swap(pair_odd, "ctx", 1).astype(F32)
    pair_terms = [swap(pair_sum[y].astype(BF), "ctx", 2 * y) for y in range(1, sides)]
    (pre_grad,) = call(
        functools.partial(join_kernel, len(pair_terms)),
        [like((length, qkv_width + LANES), BF)],
        [query_grad, pre, head_gains, cos, sin, gain_part, mid, pair_sum[0]] + pair_terms,
    )
    pre_pieces = by_mask(pre_grad)
    normed, *normed_sends = call(
        functools.partial(normed_kernel, blocks_n, qkv_rows, head_n),
        [like((quarter, width), F32)] + sends,
        [pre_grad] + qkv_args[:blocks_n],
        scratch=[pltpu.VMEM((length, width), F32)],
    )
    normed_terms = [swap(v, "head", m + 1) for m, v in enumerate(normed_sends)]
    (tokens_grad,) = call(
        functools.partial(final_kernel, head_n),
        [like((quarter, width), F32)],
        [tokens[0], gains, resid_grad, normed] + normed_terms,
    )

    slices = r // head_n
    normed_far = cross(even, odd)
    tiny_rows = 32 + max(8, -(-r // LANES))
    query_sum, key_sum, value_sum, last = call(
        functools.partial(qkv_grad_kernel, chips - 1, r, r, plane),
        [
            like((r, heads_width), F32),
            like((r, HEAD_SIZE), F32),
            like((r, HEAD_SIZE), F32),
            like((tiny_rows, LANES), F32),
        ],
        normed_far + pre_pieces + [qkv_own, prenorm[None]],
        scratch=[pltpu.VMEM((r, qkv_width), F32)],
    )
    last = sum(line_of(last))
    tiny = querynorm.shape[0] // head_n
    device = place * head_n + head_i
    prenorm_out = lax.dynamic_slice_in_dim(last[32:].reshape(-1), head_i * slices, slices, 0)
    midnorm_out = lax.dynamic_slice_in_dim(last[16:32].reshape(-1), device * slices, slices, 0)
    querynorm_out = lax.dynamic_slice_in_dim(last[0], device * tiny, tiny, 0)
    keynorm_out = lax.dynamic_slice_in_dim(last[1], device * tiny, tiny, 0)

    if wide:
        mixed_shape = like((chips, length, r + LANES), BF)
        mixed_even, mixed_odd = call(
            functools.partial(split_kernel, plane, head_n, experts, slices),
            [mixed_shape, mixed_shape],
            pieces + [inner_line],
            scratch=[
                pltpu.VMEM((length, width), BF),
                pltpu.VMEM((length, width), BF),
                pltpu.VMEM((length, LANES), F32),
            ],
        )
    else:
        order = [(head_i ^ m) for m in range(head_n)]
        stack_of = jnp.stack(pieces)
        rows_all = jnp.concatenate([lax.dynamic_index_in_dim(stack_of, o, 0, keepdims=False) for o in order], axis=0)
        line_stack = inner_line.reshape(head_n, quarter, width)
        inner_rows = jnp.concatenate([lax.dynamic_index_in_dim(line_stack, o, 0, keepdims=False) for o in order], axis=0)
        found = []
        for i in range(plane):
            mixed_block = lax.dynamic_slice_in_dim(rows_all, (place ^ i) * r, r, 1)
            near = lax.dynamic_slice_in_dim(inner_rows, (place ^ i) * r + head_i * slices, slices, 1)
            side = rows_all[:, width : width + LANES - slices]
            found.append(jnp.concatenate([mixed_block, near, side], axis=1))
        mixed_even, mixed_odd = jnp.stack(found[0::2]), jnp.stack(found[1::2])
    output_sum, small = call(
        functools.partial(output_grad_kernel, chips - 1, r, plane),
        [like((r, heads_width), F32), like((LANES, LANES), F32)],
        cross(mixed_even, mixed_odd) + by_mask(attended),
    )
    router_out = small[:slices, slices : slices + experts] + small[:slices, slices + experts : slices + 2 * experts]

    weight_sum = weight_even.astype(F32) + swap(weight_odd.astype(BF), "ctx", 1).astype(F32)
    by_part = [weight_sum[0]] + [
        swap(weight_sum[y].astype(BF), "ctx", 2 * y).astype(F32) for y in range(1, parts)
    ]
    if parts == 2:
        flip = part == 1
        by_part = [jnp.where(flip, by_part[1], by_part[0]), jnp.where(flip, by_part[0], by_part[1])]
    else:
        found = jnp.stack(by_part)
        by_part = [lax.dynamic_index_in_dim(found, part ^ j, 0, keepdims=False) for j in range(parts)]

    def expert_sum(which):
        far = jnp.stack([v[which] for v in by_part]).reshape(per_device, split, depth, columns)
        return far.transpose(2, 0, 1, 3).reshape(gate_weight.shape)

    moe_terms = [moe_back[0]] + [swap(moe_back[x], "seq", x) for x in range(1, seq_n)]
    moe, moe_sends = reduce_blocks(moe_terms, head_n)
    moe_terms = [moe] + [swap(v, "head", m + 1) for m, v in enumerate(moe_sends)]
    moe = sum(v.astype(F32) for v in moe_terms)
    out = resid + moe[:quarter]
    for y in range(1, sides):
        out = out + swap(moe[y * quarter : (y + 1) * quarter].astype(BF), "ctx", 2 * y).astype(F32)
    return (
        out.astype(BF)[None],
        tokens_grad[None],
        query_sum,
        key_sum,
        value_sum,
        output_sum,
        prenorm_out,
        midnorm_out,
        querynorm_out,
        keynorm_out,
        router_out,
        expert_sum(0),
        expert_sum(1),
        expert_sum(2),
    )


def solution(mesh):
    every = ("seq", "ctx", "head")
    expert = P("ctx", ("seq", "head"), None)
    token = P("seq", ("ctx", "head"), None)
    return jax.shard_map(
        body,
        mesh=mesh,
        in_specs=(P("seq", "ctx", None),)
        + (P(BOTH, "head"),) * 4
        + (P(BOTH),) * 4
        + (P(BOTH, None),)
        + (expert,) * 3
        + (token,) * 2,
        out_specs=(token, token)
        + (P(BOTH, "head"),) * 4
        + (P(every),) * 4
        + (P(every, None),)
        + (expert,) * 3,
        check_vma=False,
    )
```
